32 devices in a mesh: pulse: 4 (over z), tile: 8 (over y, x, core).
Axes of the slice: x: 2, y: 2, z: 4, core: 2. Of those that a mesh axis runs over, the one named last changes fastest.
Arguments:
- raw: bfloat16 [2, 128, 2048], P(None, ('pulse', 'tile')), may hold values from -6 to 6
- filt: bfloat16 [2, 1024, 2048], replicated, may hold values from -0.125 to 0.125
- range_off: int32 [128], P(('pulse', 'tile')), may hold values from 0 to 1024
- fine: int32 [128], P(('pulse', 'tile')), may hold values from 0 to 3
- dop: int32 [128], P(('pulse', 'tile')), may hold values from 0 to 511
- pulse_order: int32 [32, 4], P(('pulse', 'tile')), may hold values from 0 to 3, each once within a row
- band_idx: int32 [8, 128], P(None, ('pulse', 'tile')), may hold values from 0 to 1023
Outputs:
- image: bfloat16 [2, 512, 32768], P(None, 'pulse', 'tile')
The draws below stay inside these ranges and needn't reach their ends.
Inputs may be any that keep to these rules, and one draw needn't show every extreme that they name: `pulse_order`: each row is a permutation of 0 .. 3.
All inputs are finite; a program needn't handle non-finite values.
Results may differ from the reference program's by a relative error of at most 0.0065.
Values may be sent and summed in bfloat16 or wider, within the bound.
A program may use at most 192 MiB of HBM per device.

```python
import jax
import jax.numpy as jnp
from jax import lax

RAW = 2048
WIN = 1024
UPS = 2048
BAND = 1024
STEPS = 4
PS = 1
C_T = 4096
P_DEV = 4
PULSES = 128
ROWS = 512
N_TILE = 8
DEVICES = 32


def place_ends(result, rng, low, top_value):
    dims = result.shape
    spot = [jax.random.randint(jax.random.fold_in(rng, axis), (), 0, dims[axis]) for axis in range(len(dims))]
    result = result.at[tuple(spot)].set(low)
    longest = dims.index(max(dims))
    spot[longest] = (spot[longest] + 1) % dims[longest]
    return result.at[tuple(spot)].set(top_value)


def block_scale(key, extent, shards, smallest, top_value):
    gain, own = 1.0, jax.random.fold_in(key, 6)
    for dim, parts in shards:
        draws = jnp.exp(jax.random.uniform(jax.random.fold_in(own, dim), (parts,), jnp.float32, smallest / len(shards), top_value / len(shards)))
        gain = gain * jnp.repeat(draws, extent[dim] // parts).reshape([-1 if axis == dim else 1 for axis in range(len(extent))])
    return gain


def gaussian(stream_key, extent, deviation, most, split=(), held_as=jnp.bfloat16):
    result = deviation * jax.random.normal(stream_key, extent, jnp.float32)
    if split:
        result = result * block_scale(stream_key, extent, split, -0.22, 0.18)
    return jnp.clip(result, -most, most).astype(held_as)


def setup_inputs(seed: int = 0) -> dict:
    seeds = jax.random.split(jax.random.key(seed), 8)
    return {
        "raw": gaussian(seeds[0], (2, PULSES, RAW), 1.0, 6.0, ((1, 32),)),
        "filt": gaussian(seeds[1], (2, WIN, UPS), (2 * WIN) ** -0.5, 0.125),
        "range_off": place_ends(jax.random.randint(seeds[2], (PULSES,), 0, RAW - WIN + 1), jax.random.fold_in(seeds[2], 1), 0, RAW - WIN).astype(jnp.int32),
        "fine": place_ends(jax.random.randint(seeds[3], (PULSES,), 0, 4), jax.random.fold_in(seeds[3], 1), 0, 3).astype(jnp.int32),
        "dop": place_ends(jax.random.randint(seeds[4], (PULSES,), 0, ROWS), jax.random.fold_in(seeds[4], 1), 0, ROWS - 1).astype(jnp.int32),
        "pulse_order": jax.vmap(lambda own: jax.random.permutation(own, P_DEV))(jax.random.split(seeds[5], DEVICES)).reshape((DEVICES, P_DEV)).astype(jnp.int32),
        "band_idx": place_ends(jax.random.randint(seeds[6], (N_TILE, PULSES), 0, UPS - BAND), jax.random.fold_in(seeds[6], 1), 0, (UPS - BAND) - 1).astype(jnp.int32),
    }


def compress(windows, filt):
    wr = windows[:, 0]
    wi = windows[:, 1]
    prof_re = jnp.dot(wr, filt[0], preferred_element_type=jnp.float32) - jnp.dot(wi, filt[1], preferred_element_type=jnp.float32)
    prof_im = jnp.dot(wr, filt[1], preferred_element_type=jnp.float32) + jnp.dot(wi, filt[0], preferred_element_type=jnp.float32)
    return jnp.stack([prof_re, prof_im], 1).astype(jnp.bfloat16)

def cut_band(profile, start):
    segment = lax.dynamic_slice_in_dim(profile, start, BAND + 1, 1)
    return (segment[:, :BAND], segment[:, BAND])

def interpolate(pieces, edges, shifts):
    first = pieces.astype(jnp.float32)
    second = jnp.concatenate([first[..., 1:], edges.astype(jnp.float32)[..., None]], -1)
    first = jnp.repeat(first, 4, axis=-1)
    second = jnp.repeat(second, 4, axis=-1)
    phase_q = (jnp.arange(4 * BAND, dtype=jnp.int32) % 4).astype(jnp.float32)
    weight = (4.0 * phase_q[None, :] + shifts.astype(jnp.float32)[:, None]) / 16.0
    weight = weight[:, None, :]
    return first * (1.0 - weight) + second * weight

def reference(raw, filt, range_off, fine, dop, pulse_order, band_idx):
    devices = pulse_order.shape[0]
    p_dev = pulse_order.shape[1]
    pulses = p_dev * devices
    owners = jnp.arange(devices, dtype=jnp.int32)[:, None] * p_dev
    rows = jnp.arange(ROWS, dtype=jnp.int32)
    lefts = []
    rights = []
    for step in range(STEPS):
        chosen = (owners + pulse_order[:, step * PS:(step + 1) * PS]).reshape(-1).astype(jnp.int32)
        picked = jnp.take(raw, chosen, axis=1)
        offsets = jnp.take(range_off, chosen)
        windows = jax.vmap(lambda row, off: lax.dynamic_slice_in_dim(row, off, WIN, 1), in_axes=(1, 0))(picked, offsets)
        profile = compress(windows, filt)
        starts = jnp.take(band_idx, chosen, axis=1)
        shifts = jnp.take(fine, chosen)
        pieces, edges = jax.vmap(jax.vmap(cut_band, in_axes=(0, 0)), in_axes=(None, 0))(profile, starts)
        samples = jax.vmap(interpolate, in_axes=(0, 0, None))(pieces, edges, shifts)
        summed = lax.optimization_barrier(jnp.sum(samples, axis=1))
        sr = samples[:, :, 0]
        si = samples[:, :, 1]
        rr = summed[:, None, 0]
        ri = summed[:, None, 1]
        g_re = lax.optimization_barrier(jnp.sum(sr * rr + si * ri, axis=(0, 2)))
        g_im = lax.optimization_barrier(jnp.sum(si * rr - sr * ri, axis=(0, 2)))
        scale = jnp.sqrt(g_re * g_re + g_im * g_im + 1.0)
        c_re = (g_re / scale)[None, :, None]
        c_im = (-g_im / scale)[None, :, None]
        new_re = c_re * sr - c_im * si
        new_im = c_re * si + c_im * sr
        rights.append(jnp.concatenate([new_re, new_im], 1).astype(jnp.bfloat16))
        dops = jnp.take(dop, chosen)
        angle = 2.0 * jnp.pi * (dops[:, None] * rows[None, :] % ROWS).astype(jnp.float32) / ROWS
        e_re = (jnp.cos(angle) / jnp.sqrt(jnp.float32(pulses))).astype(jnp.bfloat16)
        e_im = (jnp.sin(angle) / jnp.sqrt(jnp.float32(pulses))).astype(jnp.bfloat16)
        lefts.append(jnp.stack([jnp.concatenate([e_re, -e_im], 0), jnp.concatenate([e_im, e_re], 0)], 0))
    left_all = jnp.concatenate(lefts, 1).astype(jnp.float32)
    right_all = jnp.concatenate(rights, 1)

    def one_tile(right):
        return jnp.einsum('zkr,kc->zrc', left_all, right.astype(jnp.float32)).astype(jnp.bfloat16)
    tiles = lax.map(one_tile, right_all)
    n_tile = tiles.shape[0]
    return jnp.transpose(tiles, (1, 2, 0, 3)).reshape(2, ROWS, n_tile * C_T)
```

```python
import functools

import jax
import jax.numpy as jnp
from jax import lax
from jax.experimental import pallas as pl
from jax.experimental.pallas import tpu as pltpu
from jax.sharding import PartitionSpec as P

F32 = jnp.float32
BF16 = jnp.bfloat16
MESH = pl.DeviceIdType.MESH
LANES = 128
DOP_SPLIT = 32
VMEM_LIMIT = 60 * 1024 * 1024


def gather_kernel(
    n_pulse, n_tile, off_ref, raw_ref, meta_ref, win_ref, all_meta_ref,
    z_send, z_recv, t_send, t_recv, p_send, p_recv,
):
    me_p = lax.axis_index("pulse")
    me_t = lax.axis_index("tile")
    half = n_tile // 2
    core = me_t % 2
    chip = me_t // 2
    partner = chip * 2 + (1 - core)
    p_dev = raw_ref.shape[0] // 2
    raw_len = raw_ref.shape[1]
    win = win_ref.shape[-1]

    def pulse_peer(d):
        return lax.rem(me_p + d, n_pulse)

    def tile_peer(d):
        return lax.rem(chip + d, half) * 2 + core

    barrier = pltpu.get_barrier_semaphore()
    for d in range(1, n_pulse):
        pl.semaphore_signal(barrier, 1, device_id=(pulse_peer(d), me_t), device_id_type=MESH)
    for d in range(1, half):
        pl.semaphore_signal(barrier, 1, device_id=(me_p, tile_peer(d)), device_id_type=MESH)
    pl.semaphore_signal(barrier, 1, device_id=(me_p, partner), device_id_type=MESH)

    raw = raw_ref[...].astype(F32)
    row = lax.broadcasted_iota(jnp.int32, (2 * p_dev, win), 0)
    cut = jnp.zeros((2 * p_dev, win), F32)
    for p in range(p_dev):
        off = off_ref[p]
        shift = jnp.where(off == 0, 0, raw_len - off)
        turned = pltpu.roll(raw, shift, 1)[:, :win]
        cut = jnp.where(row % p_dev == p, turned, cut)
    win_ref[me_p, me_t] = cut.astype(BF16)
    all_meta_ref[me_p, me_t] = meta_ref[...]
    pl.semaphore_wait(barrier, n_pulse - 1 + half - 1 + 1)

    def copies(pp, tt, send, recv, slot, target):
        return [
            pltpu.make_async_remote_copy(
                src_ref=ref.at[pp, tt],
                dst_ref=ref.at[pp, tt],
                send_sem=send.at[(a,) + slot],
                recv_sem=recv.at[(a,) + slot],
                device_id=target,
                device_id_type=MESH,
            )
            for a, ref in enumerate((win_ref, all_meta_ref))
        ]

    started = []

    def send(pp, tt, s, r, slot, target):
        for c in copies(pp, tt, s, r, slot, target):
            c.start()
            started.append(c)

    def arrive(pp, tt, s, r, slot, target):
        for c in copies(pp, tt, s, r, slot, target):
            c.wait_recv()

    for d in reversed(range(1, n_pulse)):
        send(me_p, me_t, z_send, z_recv, (d,), (pulse_peer(d), me_t))
    for dp in range(n_pulse):
        pp = lax.rem(me_p + n_pulse - dp, n_pulse)
        if dp:
            arrive(pp, me_t, z_send, z_recv, (dp,), (pulse_peer(dp), me_t))
        for dt in reversed(range(1, half)):
            send(pp, me_t, t_send, t_recv, (dp, dt), (me_p, tile_peer(dt)))
        send(pp, me_t, p_send, p_recv, (dp, 0), (me_p, partner))
    for dp in range(n_pulse):
        pp = lax.rem(me_p + n_pulse - dp, n_pulse)
        for dt in range(1, half):
            src = lax.rem(chip + half - dt, half) * 2 + core
            arrive(pp, src, t_send, t_recv, (dp, dt), (me_p, tile_peer(dt)))
            send(pp, src, p_send, p_recv, (dp, dt), (me_p, partner))
    for dp in range(n_pulse):
        pp = lax.rem(me_p + n_pulse - dp, n_pulse)
        for dt in range(half):
            src = lax.rem(chip + half - dt, half) * 2 + (1 - core)
            arrive(pp, src, p_send, p_recv, (dp, dt), (me_p, partner))
    for c in started:
        c.wait_send()


def gather(n_pulse, n_tile, range_off, raw, meta, win):
    rows = raw.shape[0]
    half = n_tile // 2
    sem = pltpu.SemaphoreType.DMA
    return pl.pallas_call(
        functools.partial(gather_kernel, n_pulse, n_tile),
        out_shape=(
            jax.ShapeDtypeStruct((n_pulse, n_tile, rows, win), BF16),
            jax.ShapeDtypeStruct((n_pulse, n_tile) + meta.shape, jnp.int32),
        ),
        in_specs=[
            pl.BlockSpec(memory_space=pltpu.SMEM),
            pl.BlockSpec(memory_space=pltpu.VMEM),
            pl.BlockSpec(memory_space=pltpu.VMEM),
        ],
        out_specs=[pl.BlockSpec(memory_space=pltpu.VMEM)] * 2,
        scratch_shapes=[
            sem((2, n_pulse)),
            sem((2, n_pulse)),
            sem((2, n_pulse, half)),
            sem((2, n_pulse, half)),
            sem((2, n_pulse, half)),
            sem((2, n_pulse, half)),
        ],
        compiler_params=pltpu.CompilerParams(collective_id=0, has_side_effects=True),
    )(range_off, raw, meta)


def spread(meta, field, rows8, n_rows):
    lane = lax.broadcasted_iota(jnp.int32, (meta.shape[1], n_rows), 0)
    col = lax.broadcasted_iota(jnp.int32, (meta.shape[1], n_rows), 1)
    pick = (lane == field * rows8 + col % rows8).astype(F32).astype(BF16)
    wide = jnp.dot(meta, pick, preferred_element_type=F32)
    owner = lax.broadcasted_iota(jnp.int32, wide.shape, 0)
    column = lax.broadcasted_iota(jnp.int32, wide.shape, 1)
    return jnp.sum(jnp.where(owner == column // rows8, wide, 0.0), axis=0, keepdims=True)


def thirds(x):
    a = x.astype(BF16)
    rest = x - a.astype(F32)
    b = rest.astype(BF16)
    return [a, b, (rest - b.astype(F32)).astype(BF16)]


def swap_parts(v, part1, p_dev):
    n = v.shape[-1]
    return jnp.where(part1, pltpu.roll(v, p_dev, 1), pltpu.roll(v, n - p_dev, 1))


def compress_kernel(
    steps, p_dev, idx_ref, meta_ref, win_ref, filt_ref,
    bands_ref, g_ref, vec_ref, x_ref, prof_ref, cut_ref,
):
    i = pl.program_id(0)
    n_rows, win = x_ref.shape[1:]
    rows8 = 2 * p_dev
    n_dev = n_rows // rows8
    chunk = filt_ref.shape[2]
    band = bands_ref.shape[1]
    pieces = band // LANES

    @pl.when(i == 0)
    def _():
        x = win_ref[...].astype(F32)
        r = lax.broadcasted_iota(jnp.int32, x.shape, 1)
        y = jnp.where(r < p_dev, -1.0, 1.0) * pltpu.roll(x, p_dev, 1)
        x_ref[0] = x.reshape(n_rows, win).astype(BF16)
        x_ref[1] = y.reshape(n_rows, win).astype(BF16)

    acc = jnp.dot(x_ref[0], filt_ref[0], preferred_element_type=F32) + jnp.dot(
        x_ref[1], filt_ref[1], preferred_element_type=F32
    )
    acc = acc.astype(BF16).astype(F32)
    stride = prof_ref.shape[0] // n_rows
    for c in range(chunk // LANES):
        prof_ref[pl.ds(i * (chunk // LANES) + c, n_rows, stride=stride), :] = acc[
            :, c * LANES : (c + 1) * LANES
        ]

    @pl.when(i == pl.num_programs(0) - 1)
    def _():
        tile = lax.axis_index("tile")
        lane = lax.broadcasted_iota(jnp.int32, (pieces, LANES), 1)

        def cut_owner(d, carry):
            for p in range(p_dev):
                start = idx_ref[d, 4 * rows8 + tile * p_dev + p]
                for b in range(2):
                    s = start + b
                    q = s // LANES
                    r = s % LANES
                    turn = jnp.where(r == 0, 0, LANES - r)
                    for part in range(2):
                        row = d * rows8 + part * p_dev + p
                        low = prof_ref[pl.ds(row * stride + q, pieces), :]
                        high = prof_ref[pl.ds(row * stride + q + 1, pieces), :]
                        cut_ref[pl.ds((b * n_rows + row) * pieces, pieces), :] = jnp.where(
                            lane < LANES - r, pltpu.roll(low, turn, 1), pltpu.roll(high, turn, 1)
                        )
            return carry

        lax.fori_loop(0, n_dev, cut_owner, 0)
        for c in range(pieces):
            bands_ref[:, c * LANES : (c + 1) * LANES] = cut_ref[
                pl.ds(c, 2 * n_rows, stride=pieces), :
            ].astype(BF16)

        meta = meta_ref[...].astype(F32).astype(BF16)
        blk = spread(meta, 0, rows8, n_rows)
        fine = spread(meta, 1, rows8, n_rows) * (1.0 / 16.0)
        dop = spread(meta, 2, rows8, n_rows) + DOP_SPLIT * spread(meta, 3, rows8, n_rows)
        sel = lax.broadcasted_iota(jnp.int32, (2 * steps, n_rows), 0)
        col = lax.broadcasted_iota(jnp.int32, (2 * steps, n_rows), 1)
        mine = ((sel // 2).astype(F32) == blk) & (sel % 2 == (col % rows8) // p_dev)
        zero = jnp.zeros((2 * steps, n_rows), F32)
        p_left = jnp.concatenate([jnp.where(mine, 1.0 - fine, zero), jnp.where(mine, fine, zero)], 1)
        q_left = jnp.concatenate([jnp.where(mine, -1.0, zero), jnp.where(mine, 1.0, zero)], 1)
        left = jnp.concatenate([p_left, q_left], 0).astype(BF16)
        pq = jnp.dot(left, bands_ref[...], preferred_element_type=F32)
        p_sum = pq[: 2 * steps]
        q_sum = pq[2 * steps :]
        x = 4.0 * p_sum + 1.5 * q_sum
        y = 1.5 * p_sum + 0.875 * q_sum
        xs = jnp.concatenate(thirds(x) + thirds(y), 0)
        d6 = lax.dot_general(
            xs, bands_ref[...], (((1,), (1,)), ((), ())), preferred_element_type=F32
        )
        k = 2 * steps
        dx = d6[2 * k : 3 * k] + d6[k : 2 * k] + d6[:k]
        dy = d6[5 * k : 6 * k] + d6[4 * k : 5 * k] + d6[3 * k : 4 * k]
        h = ((1.0 - fine) * dx[:, :n_rows] - dy[:, :n_rows]) + (
            fine * dx[:, n_rows:] + dy[:, n_rows:]
        )
        in_block = (sel // 2).astype(F32) == blk
        hr = jnp.sum(jnp.where(in_block & (sel % 2 == 0), h, 0.0), axis=0, keepdims=True)
        hi = jnp.sum(jnp.where(in_block & (sel % 2 == 1), h, 0.0), axis=0, keepdims=True)
        both = jnp.concatenate([hr, hi, jnp.zeros((6, n_rows), F32)], 0)
        part1 = (lax.broadcasted_iota(jnp.int32, (8, n_rows), 1) % rows8) >= p_dev
        other = swap_parts(both, part1, p_dev)
        hr, hi, hr_o, hi_o = both[0:1], both[1:2], other[0:1], other[1:2]
        one = part1[0:1]
        g_ref[0:1] = jnp.where(one, hr_o + hi, hr + hi_o)
        g_ref[1:2] = jnp.where(one, hr - hi_o, hr_o - hi)
        vec_ref[...] = jnp.concatenate([fine, dop, jnp.zeros((6, n_rows), F32)], 0)


def compress_all(steps, p_dev, meta, windows, filt, band):
    n_dev, rows8, win = windows.shape
    n_rows = n_dev * rows8
    ups = filt.shape[2]
    chunk = 2 * LANES
    chunks = ups // LANES
    pieces = band // LANES
    grid_spec = pltpu.PrefetchScalarGridSpec(
        num_scalar_prefetch=1,
        grid=(ups // chunk,),
        in_specs=[
            pl.BlockSpec(meta.shape, lambda i, s: (0, 0)),
            pl.BlockSpec(windows.shape, lambda i, s: (0, 0, 0)),
            pl.BlockSpec((2, win, chunk), lambda i, s: (0, 0, i)),
        ],
        out_specs=[
            pl.BlockSpec((2 * n_rows, band), lambda i, s: (0, 0)),
            pl.BlockSpec((2, n_rows), lambda i, s: (0, 0)),
            pl.BlockSpec((8, n_rows), lambda i, s: (0, 0)),
        ],
        scratch_shapes=[
            pltpu.VMEM((2, n_rows, win), BF16),
            pltpu.VMEM((n_rows * chunks + 8, LANES), F32),
            pltpu.VMEM((2 * n_rows * pieces, LANES), F32),
        ],
    )
    return pl.pallas_call(
        functools.partial(compress_kernel, steps, p_dev),
        out_shape=(
            jax.ShapeDtypeStruct((2 * n_rows, band), BF16),
            jax.ShapeDtypeStruct((2, n_rows), F32),
            jax.ShapeDtypeStruct((8, n_rows), F32),
        ),
        grid_spec=grid_spec,
        compiler_params=pltpu.CompilerParams(vmem_limit_bytes=VMEM_LIMIT),
    )(meta, meta, windows, filt)


def focus_kernel(n_pulse, n_tile, r_dev, p_dev, g_ref, vec_ref, left_ref, got_ref, send_sem, recv_sem):
    me_p = lax.axis_index("pulse")
    me_t = lax.axis_index("tile")
    n_rows = g_ref.shape[1]
    rows8 = 2 * p_dev
    total_rows = r_dev * n_pulse
    pulses = n_rows // 2
    barrier = pltpu.get_barrier_semaphore()

    def peer(d):
        return (me_p, lax.rem(me_t + d, n_tile))

    for d in range(1, n_tile):
        pl.semaphore_signal(barrier, 1, device_id=peer(d), device_id_type=MESH)
    pl.semaphore_wait(barrier, n_tile - 1)
    moves = [
        pltpu.make_async_remote_copy(
            src_ref=g_ref,
            dst_ref=got_ref.at[d],
            send_sem=send_sem.at[d],
            recv_sem=recv_sem.at[d],
            device_id=peer(d),
            device_id_type=MESH,
        )
        for d in range(1, n_tile)
    ]
    for move in moves:
        move.start()
    fine = vec_ref[0:1]
    dop = vec_ref[1:2].astype(jnp.int32)
    row = me_p * r_dev + lax.broadcasted_iota(jnp.int32, (r_dev, n_rows), 0)
    angle = 2.0 * jnp.pi * ((dop * row) & (total_rows - 1)).astype(F32) / total_rows
    norm = 1.0 / jnp.sqrt(F32(pulses))
    er = (jnp.cos(angle) * norm).astype(BF16).astype(F32)
    ei = (jnp.sin(angle) * norm).astype(BF16).astype(F32)
    total = g_ref[...]
    for d in range(1, n_tile):
        moves[d - 1].wait_recv()
        total = total + got_ref[d]
    g_re, g_im = total[0:1], total[1:2]
    scale = jnp.sqrt(g_re * g_re + g_im * g_im + 1.0)
    c_re = g_re / scale
    c_im = -g_im / scale
    one = (lax.broadcasted_iota(jnp.int32, (1, n_rows), 1) % rows8) >= p_dev
    alpha = jnp.where(one, -c_im, c_re)
    beta = jnp.where(one, c_re, c_im)
    w = (er * alpha - ei * beta, er * beta + ei * alpha)
    for z in range(2):
        here = pl.ds(z * r_dev, r_dev)
        left_ref[0, here, :n_rows] = (w[z] * (1.0 - fine)).astype(BF16)
        left_ref[0, here, n_rows:] = (w[z] * fine).astype(BF16)
        left_ref[1, here, :n_rows] = (w[z] * -fine).astype(BF16)
        left_ref[1, here, n_rows:] = (w[z] * (1.0 + fine)).astype(BF16)
    for move in moves:
        move.wait_send()


def focus(n_pulse, n_tile, r_dev, p_dev, g, vec):
    n_rows = g.shape[1]
    return pl.pallas_call(
        functools.partial(focus_kernel, n_pulse, n_tile, r_dev, p_dev),
        out_shape=jax.ShapeDtypeStruct((2, 2 * r_dev, 2 * n_rows), BF16),
        in_specs=[pl.BlockSpec(memory_space=pltpu.VMEM)] * 2,
        out_specs=pl.BlockSpec(memory_space=pltpu.VMEM),
        scratch_shapes=[
            pltpu.VMEM((n_tile,) + g.shape, F32),
            pltpu.SemaphoreType.DMA((n_tile,)),
            pltpu.SemaphoreType.DMA((n_tile,)),
        ],
        compiler_params=pltpu.CompilerParams(
            collective_id=1, has_side_effects=True, vmem_limit_bytes=VMEM_LIMIT
        ),
    )(g, vec)


def image_kernel(left_ref, bands_ref, out_ref, up_ref):
    r_dev = out_ref.shape[1]
    width = bands_ref.shape[1]
    out_chunk = 4 * LANES
    j = lax.broadcasted_iota(jnp.int32, up_ref.shape, 0)
    c = lax.broadcasted_iota(jnp.int32, up_ref.shape, 1)
    w = (c % 4).astype(F32) * 0.25
    up = jnp.where(j < LANES, 1.0 - w, w)
    up_ref[...] = jnp.where(j % LANES == c // 4, up, 0.0).astype(BF16)
    r0 = jnp.dot(left_ref[0], bands_ref[...], preferred_element_type=F32).astype(BF16)
    r1 = jnp.dot(left_ref[1], bands_ref[...], preferred_element_type=F32).astype(BF16)
    for s in range(width // LANES):
        cols = slice(s * LANES, (s + 1) * LANES)
        both = jnp.concatenate([r0[:, cols], r1[:, cols]], 1)
        res = jnp.dot(both, up_ref[...], preferred_element_type=F32).astype(BF16)
        for z in range(2):
            out_ref[z, :, s * out_chunk : (s + 1) * out_chunk] = res[z * r_dev : (z + 1) * r_dev]


def image(left, bands, r_dev):
    band = bands.shape[1]
    k = bands.shape[0]
    width = 2 * LANES
    return pl.pallas_call(
        image_kernel,
        grid=(band // width,),
        out_shape=jax.ShapeDtypeStruct((2, r_dev, 4 * band), BF16),
        in_specs=[
            pl.BlockSpec(left.shape, lambda i: (0, 0, 0)),
            pl.BlockSpec((k, width), lambda i: (0, i)),
        ],
        out_specs=pl.BlockSpec((2, r_dev, 4 * width), lambda i: (0, 0, i)),
        scratch_shapes=[pltpu.VMEM((2 * LANES, 4 * LANES), BF16)],
        compiler_params=pltpu.CompilerParams(vmem_limit_bytes=VMEM_LIMIT),
    )(left, bands)


BAND = 1024
R_DEV = 128


def shards(raw, filt, range_off, fine, dop, pulse_order, band_idx):
    n_pulse = lax.axis_size("pulse")
    n_tile = lax.axis_size("tile")
    p_dev = raw.shape[1]
    win = filt.shape[1]
    steps = pulse_order.shape[1]
    order = pulse_order[0]
    ids = jnp.arange(p_dev, dtype=jnp.int32)
    slot = jnp.arange(steps, dtype=jnp.int32)
    blk = jnp.sum(jnp.where(order[None, :] == ids[:, None], slot[None, :], 0), axis=1)
    meta = jnp.concatenate(
        [
            blk, blk, fine, fine,
            dop % DOP_SPLIT, dop % DOP_SPLIT, dop // DOP_SPLIT, dop // DOP_SPLIT,
            band_idx.reshape(-1),
        ]
    )
    meta = jnp.pad(meta, (0, -meta.shape[0] % LANES))[None]
    windows, all_meta = gather(
        n_pulse, n_tile, range_off, raw.reshape(2 * p_dev, -1), meta, win
    )
    n_dev = n_pulse * n_tile
    windows = windows.reshape(n_dev, 2 * p_dev, win)
    all_meta = all_meta.reshape(n_dev, -1)
    bands, g, vec = compress_all(steps, p_dev, all_meta, windows, filt, BAND)
    left = focus(n_pulse, n_tile, R_DEV, p_dev, g, vec)
    return image(left, bands, R_DEV)


def solution(mesh):
    return jax.shard_map(
        shards,
        mesh=mesh,
        in_specs=(
            P(None, ("pulse", "tile"), None),
            P(),
            P(("pulse", "tile")),
            P(("pulse", "tile")),
            P(("pulse", "tile")),
            P(("pulse", "tile"), None),
            P(None, ("pulse", "tile")),
        ),
        out_specs=P(None, "pulse", "tile"),
        check_vma=False,
    )
```

```python
import functools

import jax
import jax.numpy as jnp
from jax import lax
from jax.experimental import pallas as pl
from jax.experimental.pallas import tpu as pltpu
from jax.sharding import PartitionSpec as P

F32 = jnp.float32
BF16 = jnp.bfloat16
MESH = pl.DeviceIdType.MESH
LANES = 128
DOP_SPLIT = 32
VMEM_LIMIT = 60 * 1024 * 1024


def gather_kernel(
    n_pulse, n_tile, off_ref, fine_ref, dop_ref, order_ref, idx_ref, raw_ref, win_ref, all_meta_ref,
    z_send, z_recv, t_send, t_recv, p_send, p_recv,
):
    me_p = lax.axis_index("pulse")
    me_t = lax.axis_index("tile")
    half = n_tile // 2
    core = me_t % 2
    chip = me_t // 2
    partner = chip * 2 + (1 - core)
    p_dev = raw_ref.shape[1]
    raw_len = raw_ref.shape[2]
    win = win_ref.shape[-1]

    def pulse_peer(d):
        return lax.rem(me_p + d, n_pulse)

    def tile_peer(d):
        return lax.rem(chip + d, half) * 2 + core

    barrier = pltpu.get_barrier_semaphore()
    for d in range(1, n_pulse):
        pl.semaphore_signal(barrier, 1, device_id=(pulse_peer(d), me_t), device_id_type=MESH)
    for d in range(1, half):
        pl.semaphore_signal(barrier, 1, device_id=(me_p, tile_peer(d)), device_id_type=MESH)
    pl.semaphore_signal(barrier, 1, device_id=(me_p, partner), device_id_type=MESH)

    raw = jnp.concatenate([raw_ref[0].astype(F32), raw_ref[1].astype(F32)], 0)
    row = lax.broadcasted_iota(jnp.int32, (2 * p_dev, win), 0)
    cut = jnp.zeros((2 * p_dev, win), F32)
    for p in range(p_dev):
        off = off_ref[p]
        shift = jnp.where(off == 0, 0, raw_len - off)
        turned = pltpu.roll(raw, shift, 1)[:, :win]
        cut = jnp.where(row % p_dev == p, turned, cut)
    win_ref[me_p, me_t] = cut.astype(BF16)
    lane = lax.broadcasted_iota(jnp.int32, all_meta_ref.shape[2:], 1)
    line = jnp.zeros(all_meta_ref.shape[2:], jnp.int32)
    rows8 = 2 * p_dev
    for p in range(p_dev):
        pulse_lane = (lane < 4 * rows8) & (lane % p_dev == p)
        line = jnp.where(pulse_lane & (lane // rows8 == 1), fine_ref[p], line)
        line = jnp.where(pulse_lane & (lane // rows8 == 2), dop_ref[p] % DOP_SPLIT, line)
        line = jnp.where(pulse_lane & (lane // rows8 == 3), dop_ref[p] // DOP_SPLIT, line)
        line = jnp.where((lane < rows8) & (lane % p_dev == order_ref[0, p]), p, line)
        for t in range(n_tile):
            line = jnp.where(lane == 4 * rows8 + t * p_dev + p, idx_ref[t, p], line)
    all_meta_ref[me_p, me_t] = line
    pl.semaphore_wait(barrier, n_pulse - 1 + half - 1 + 1)

    def copies(pp, tt, send, recv, slot, target):
        return [
            pltpu.make_async_remote_copy(
                src_ref=ref.at[pp, tt],
                dst_ref=ref.at[pp, tt],
                send_sem=send.at[(a,) + slot],
                recv_sem=recv.at[(a,) + slot],
                device_id=target,
                device_id_type=MESH,
            )
            for a, ref in enumerate((win_ref, all_meta_ref))
        ]

    started = []

    def send(pp, tt, s, r, slot, target):
        for c in copies(pp, tt, s, r, slot, target):
            c.start()
            started.append(c)

    def arrive(pp, tt, s, r, slot, target):
        for c in copies(pp, tt, s, r, slot, target):
            c.wait_recv()

    for d in reversed(range(1, n_pulse)):
        send(me_p, me_t, z_send, z_recv, (d,), (pulse_peer(d), me_t))
    for dp in range(n_pulse):
        pp = lax.rem(me_p + n_pulse - dp, n_pulse)
        if dp:
            arrive(pp, me_t, z_send, z_recv, (dp,), (pulse_peer(dp), me_t))
        for dt in reversed(range(1, half)):
            send(pp, me_t, t_send, t_recv, (dp, dt), (me_p, tile_peer(dt)))
        send(pp, me_t, p_send, p_recv, (dp, 0), (me_p, partner))
    for dp in range(n_pulse):
        pp = lax.rem(me_p + n_pulse - dp, n_pulse)
        for dt in range(1, half):
            src = lax.rem(chip + half - dt, half) * 2 + core
            arrive(pp, src, t_send, t_recv, (dp, dt), (me_p, tile_peer(dt)))
            send(pp, src, p_send, p_recv, (dp, dt), (me_p, partner))
    for dp in range(n_pulse):
        pp = lax.rem(me_p + n_pulse - dp, n_pulse)
        for dt in range(half):
            src = lax.rem(chip + half - dt, half) * 2 + (1 - core)
            arrive(pp, src, p_send, p_recv, (dp, dt), (me_p, partner))
    for c in started:
        c.wait_send()


def gather(n_pulse, n_tile, range_off, fine, dop, order, idx, raw, win):
    rows = 2 * raw.shape[1]
    fields = 4 * rows + idx.size
    width = fields + -fields % LANES
    half = n_tile // 2
    sem = pltpu.SemaphoreType.DMA
    return pl.pallas_call(
        functools.partial(gather_kernel, n_pulse, n_tile),
        out_shape=(
            jax.ShapeDtypeStruct((n_pulse, n_tile, rows, win), BF16),
            jax.ShapeDtypeStruct((n_pulse, n_tile, 1, width), jnp.int32),
        ),
        in_specs=[pl.BlockSpec(memory_space=pltpu.SMEM)] * 5
        + [pl.BlockSpec(memory_space=pltpu.VMEM)],
        out_specs=[pl.BlockSpec(memory_space=pltpu.VMEM)] * 2,
        scratch_shapes=[
            sem((2, n_pulse)),
            sem((2, n_pulse)),
            sem((2, n_pulse, half)),
            sem((2, n_pulse, half)),
            sem((2, n_pulse, half)),
            sem((2, n_pulse, half)),
        ],
        compiler_params=pltpu.CompilerParams(collective_id=0, has_side_effects=True),
    )(range_off, fine, dop, order, idx, raw)


def spread(meta, field, rows8, n_rows):
    lane = lax.broadcasted_iota(jnp.int32, (meta.shape[1], n_rows), 0)
    col = lax.broadcasted_iota(jnp.int32, (meta.shape[1], n_rows), 1)
    pick = (lane == field * rows8 + col % rows8).astype(F32).astype(BF16)
    wide = jnp.dot(meta, pick, preferred_element_type=F32)
    owner = lax.broadcasted_iota(jnp.int32, wide.shape, 0)
    column = lax.broadcasted_iota(jnp.int32, wide.shape, 1)
    return jnp.sum(jnp.where(owner == column // rows8, wide, 0.0), axis=0, keepdims=True)


def thirds(x):
    a = x.astype(BF16)
    rest = x - a.astype(F32)
    b = rest.astype(BF16)
    return [a, b, (rest - b.astype(F32)).astype(BF16)]


def swap_parts(v, part1, p_dev):
    n = v.shape[-1]
    return jnp.where(part1, pltpu.roll(v, p_dev, 1), pltpu.roll(v, n - p_dev, 1))


def compress_kernel(
    steps, p_dev, idx_ref, meta_ref, win_ref, filt_ref,
    bands_ref, g_ref, vec_ref, x_ref, prof_ref, cut_ref,
):
    i = pl.program_id(0)
    n_rows, win = x_ref.shape[1:]
    rows8 = 2 * p_dev
    n_dev = n_rows // rows8
    chunk = filt_ref.shape[2]
    band = bands_ref.shape[1]
    pieces = band // LANES

    @pl.when(i == 0)
    def _():
        x = win_ref[...].astype(F32)
        r = lax.broadcasted_iota(jnp.int32, x.shape, 1)
        y = jnp.where(r < p_dev, -1.0, 1.0) * pltpu.roll(x, p_dev, 1)
        x_ref[0] = x.reshape(n_rows, win).astype(BF16)
        x_ref[1] = y.reshape(n_rows, win).astype(BF16)

    acc = jnp.dot(x_ref[0], filt_ref[0], preferred_element_type=F32) + jnp.dot(
        x_ref[1], filt_ref[1], preferred_element_type=F32
    )
    acc = acc.astype(BF16).astype(F32)
    stride = prof_ref.shape[0] // n_rows
    for c in range(chunk // LANES):
        prof_ref[pl.ds(i * (chunk // LANES) + c, n_rows, stride=stride), :] = acc[
            :, c * LANES : (c + 1) * LANES
        ]

    @pl.when(i == pl.num_programs(0) - 1)
    def _():
        tile = lax.axis_index("tile")
        lane = lax.broadcasted_iota(jnp.int32, (pieces, LANES), 1)

        def cut_owner(d, carry):
            for p in range(p_dev):
                start = idx_ref[d, 4 * rows8 + tile * p_dev + p]
                for b in range(2):
                    s = start + b
                    q = s // LANES
                    r = s % LANES
                    turn = jnp.where(r == 0, 0, LANES - r)
                    for part in range(2):
                        row = d * rows8 + part * p_dev + p
                        low = prof_ref[pl.ds(row * stride + q, pieces), :]
                        high = prof_ref[pl.ds(row * stride + q + 1, pieces), :]
                        cut_ref[pl.ds((b * n_rows + row) * pieces, pieces), :] = jnp.where(
                            lane < LANES - r, pltpu.roll(low, turn, 1), pltpu.roll(high, turn, 1)
                        )
            return carry

        lax.fori_loop(0, n_dev, cut_owner, 0, unroll=4)
        for c in range(pieces):
            bands_ref[:, c * LANES : (c + 1) * LANES] = cut_ref[
                pl.ds(c, 2 * n_rows, stride=pieces), :
            ].astype(BF16)

        meta = meta_ref[...].astype(F32).astype(BF16)
        blk = spread(meta, 0, rows8, n_rows)
        fine = spread(meta, 1, rows8, n_rows) * (1.0 / 16.0)
        dop = spread(meta, 2, rows8, n_rows) + DOP_SPLIT * spread(meta, 3, rows8, n_rows)
        sel = lax.broadcasted_iota(jnp.int32, (2 * steps, n_rows), 0)
        col = lax.broadcasted_iota(jnp.int32, (2 * steps, n_rows), 1)
        mine = ((sel // 2).astype(F32) == blk) & (sel % 2 == (col % rows8) // p_dev)
        zero = jnp.zeros((2 * steps, n_rows), F32)
        p_left = jnp.concatenate([jnp.where(mine, 1.0 - fine, zero), jnp.where(mine, fine, zero)], 1)
        q_left = jnp.concatenate([jnp.where(mine, -1.0, zero), jnp.where(mine, 1.0, zero)], 1)
        left = jnp.concatenate([p_left, q_left], 0).astype(BF16)
        pq = jnp.dot(left, bands_ref[...], preferred_element_type=F32)
        p_sum = pq[: 2 * steps]
        q_sum = pq[2 * steps :]
        x = 4.0 * p_sum + 1.5 * q_sum
        y = 1.5 * p_sum + 0.875 * q_sum
        xs = jnp.concatenate(thirds(x) + thirds(y), 0)
        d6 = lax.dot_general(
            xs, bands_ref[...], (((1,), (1,)), ((), ())), preferred_element_type=F32
        )
        k = 2 * steps
        dx = d6[2 * k : 3 * k] + d6[k : 2 * k] + d6[:k]
        dy = d6[5 * k : 6 * k] + d6[4 * k : 5 * k] + d6[3 * k : 4 * k]
        h = ((1.0 - fine) * dx[:, :n_rows] - dy[:, :n_rows]) + (
            fine * dx[:, n_rows:] + dy[:, n_rows:]
        )
        in_block = (sel // 2).astype(F32) == blk
        hr = jnp.sum(jnp.where(in_block & (sel % 2 == 0), h, 0.0), axis=0, keepdims=True)
        hi = jnp.sum(jnp.where(in_block & (sel % 2 == 1), h, 0.0), axis=0, keepdims=True)
        both = jnp.concatenate([hr, hi, jnp.zeros((6, n_rows), F32)], 0)
        part1 = (lax.broadcasted_iota(jnp.int32, (8, n_rows), 1) % rows8) >= p_dev
        other = swap_parts(both, part1, p_dev)
        hr, hi, hr_o, hi_o = both[0:1], both[1:2], other[0:1], other[1:2]
        one = part1[0:1]
        g_ref[0:1] = jnp.where(one, hr_o + hi, hr + hi_o)
        g_ref[1:2] = jnp.where(one, hr - hi_o, hr_o - hi)
        vec_ref[...] = jnp.concatenate([fine, dop, jnp.zeros((6, n_rows), F32)], 0)


def compress_all(steps, p_dev, meta, windows, filt, band):
    n_dev, rows8, win = windows.shape
    n_rows = n_dev * rows8
    ups = filt.shape[2]
    chunk = 2 * LANES
    chunks = ups // LANES
    pieces = band // LANES
    grid_spec = pltpu.PrefetchScalarGridSpec(
        num_scalar_prefetch=1,
        grid=(ups // chunk,),
        in_specs=[
            pl.BlockSpec(meta.shape, lambda i, s: (0, 0)),
            pl.BlockSpec(windows.shape, lambda i, s: (0, 0, 0)),
            pl.BlockSpec((2, win, chunk), lambda i, s: (0, 0, i)),
        ],
        out_specs=[
            pl.BlockSpec((2 * n_rows, band), lambda i, s: (0, 0)),
            pl.BlockSpec((2, n_rows), lambda i, s: (0, 0)),
            pl.BlockSpec((8, n_rows), lambda i, s: (0, 0)),
        ],
        scratch_shapes=[
            pltpu.VMEM((2, n_rows, win), BF16),
            pltpu.VMEM((n_rows * chunks + 8, LANES), F32),
            pltpu.VMEM((2 * n_rows * pieces, LANES), F32),
        ],
    )
    return pl.pallas_call(
        functools.partial(compress_kernel, steps, p_dev),
        out_shape=(
            jax.ShapeDtypeStruct((2 * n_rows, band), BF16),
            jax.ShapeDtypeStruct((2, n_rows), F32),
            jax.ShapeDtypeStruct((8, n_rows), F32),
        ),
        grid_spec=grid_spec,
        compiler_params=pltpu.CompilerParams(vmem_limit_bytes=VMEM_LIMIT),
    )(meta, meta, windows, filt)


def focus_kernel(n_pulse, n_tile, r_dev, p_dev, g_ref, vec_ref, left_ref, got_ref, send_sem, recv_sem):
    me_p = lax.axis_index("pulse")
    me_t = lax.axis_index("tile")
    n_rows = g_ref.shape[1]
    rows8 = 2 * p_dev
    total_rows = r_dev * n_pulse
    pulses = n_rows // 2
    barrier = pltpu.get_barrier_semaphore()

    def peer(d):
        return (me_p, lax.rem(me_t + d, n_tile))

    for d in range(1, n_tile):
        pl.semaphore_signal(barrier, 1, device_id=peer(d), device_id_type=MESH)
    pl.semaphore_wait(barrier, n_tile - 1)
    moves = [
        pltpu.make_async_remote_copy(
            src_ref=g_ref,
            dst_ref=got_ref.at[d],
            send_sem=send_sem.at[d],
            recv_sem=recv_sem.at[d],
            device_id=peer(d),
            device_id_type=MESH,
        )
        for d in range(1, n_tile)
    ]
    for move in moves:
        move.start()
    fine = vec_ref[0:1]
    dop = vec_ref[1:2].astype(jnp.int32)
    row = me_p * r_dev + lax.broadcasted_iota(jnp.int32, (r_dev, n_rows), 0)
    angle = 2.0 * jnp.pi * ((dop * row) & (total_rows - 1)).astype(F32) / total_rows
    norm = 1.0 / jnp.sqrt(F32(pulses))
    er = (jnp.cos(angle) * norm).astype(BF16).astype(F32)
    ei = (jnp.sin(angle) * norm).astype(BF16).astype(F32)
    total = g_ref[...]
    for d in range(1, n_tile):
        moves[d - 1].wait_recv()
        total = total + got_ref[d]
    g_re, g_im = total[0:1], total[1:2]
    scale = jnp.sqrt(g_re * g_re + g_im * g_im + 1.0)
    c_re = g_re / scale
    c_im = -g_im / scale
    one = (lax.broadcasted_iota(jnp.int32, (1, n_rows), 1) % rows8) >= p_dev
    alpha = jnp.where(one, -c_im, c_re)
    beta = jnp.where(one, c_re, c_im)
    w = (er * alpha - ei * beta, er * beta + ei * alpha)
    for z in range(2):
        here = pl.ds(z * r_dev, r_dev)
        left_ref[0, here, :n_rows] = (w[z] * (1.0 - fine)).astype(BF16)
        left_ref[0, here, n_rows:] = (w[z] * fine).astype(BF16)
        left_ref[1, here, :n_rows] = (w[z] * -fine).astype(BF16)
        left_ref[1, here, n_rows:] = (w[z] * (1.0 + fine)).astype(BF16)
    for move in moves:
        move.wait_send()


def focus(n_pulse, n_tile, r_dev, p_dev, g, vec):
    n_rows = g.shape[1]
    return pl.pallas_call(
        functools.partial(focus_kernel, n_pulse, n_tile, r_dev, p_dev),
        out_shape=jax.ShapeDtypeStruct((2, 2 * r_dev, 2 * n_rows), BF16),
        in_specs=[pl.BlockSpec(memory_space=pltpu.VMEM)] * 2,
        out_specs=pl.BlockSpec(memory_space=pltpu.VMEM),
        scratch_shapes=[
            pltpu.VMEM((n_tile,) + g.shape, F32),
            pltpu.SemaphoreType.DMA((n_tile,)),
            pltpu.SemaphoreType.DMA((n_tile,)),
        ],
        compiler_params=pltpu.CompilerParams(
            collective_id=1, has_side_effects=True, vmem_limit_bytes=VMEM_LIMIT
        ),
    )(g, vec)


def image_kernel(left_ref, bands_ref, out_ref, up_ref):
    r_dev = out_ref.shape[1]
    width = bands_ref.shape[1]
    out_chunk = 4 * LANES
    j = lax.broadcasted_iota(jnp.int32, up_ref.shape, 0)
    c = lax.broadcasted_iota(jnp.int32, up_ref.shape, 1)
    w = (c % 4).astype(F32) * 0.25
    up = jnp.where(j < LANES, 1.0 - w, w)
    up_ref[...] = jnp.where(j % LANES == c // 4, up, 0.0).astype(BF16)
    r0 = jnp.dot(left_ref[0], bands_ref[...], preferred_element_type=F32).astype(BF16)
    r1 = jnp.dot(left_ref[1], bands_ref[...], preferred_element_type=F32).astype(BF16)
    for s in range(width // LANES):
        cols = slice(s * LANES, (s + 1) * LANES)
        both = jnp.concatenate([r0[:, cols], r1[:, cols]], 1)
        res = jnp.dot(both, up_ref[...], preferred_element_type=F32).astype(BF16)
        for z in range(2):
            out_ref[z, :, s * out_chunk : (s + 1) * out_chunk] = res[z * r_dev : (z + 1) * r_dev]


def image(left, bands, r_dev):
    band = bands.shape[1]
    k = bands.shape[0]
    width = 2 * LANES
    return pl.pallas_call(
        image_kernel,
        grid=(band // width,),
        out_shape=jax.ShapeDtypeStruct((2, r_dev, 4 * band), BF16),
        in_specs=[
            pl.BlockSpec(left.shape, lambda i: (0, 0, 0)),
            pl.BlockSpec((k, width), lambda i: (0, i)),
        ],
        out_specs=pl.BlockSpec((2, r_dev, 4 * width), lambda i: (0, 0, i)),
        scratch_shapes=[pltpu.VMEM((2 * LANES, 4 * LANES), BF16)],
        compiler_params=pltpu.CompilerParams(vmem_limit_bytes=VMEM_LIMIT),
    )(left, bands)


BAND = 1024
R_DEV = 128


def shards(raw, filt, range_off, fine, dop, pulse_order, band_idx):
    n_pulse = lax.axis_size("pulse")
    n_tile = lax.axis_size("tile")
    p_dev = raw.shape[1]
    win = filt.shape[1]
    steps = pulse_order.shape[1]
    windows, all_meta = gather(
        n_pulse, n_tile, range_off, fine, dop, pulse_order, band_idx, raw, win
    )
    n_dev = n_pulse * n_tile
    windows = windows.reshape(n_dev, 2 * p_dev, win)
    all_meta = all_meta.reshape(n_dev, -1)
    bands, g, vec = compress_all(steps, p_dev, all_meta, windows, filt, BAND)
    left = focus(n_pulse, n_tile, R_DEV, p_dev, g, vec)
    return image(left, bands, R_DEV)


def solution(mesh):
    return jax.shard_map(
        shards,
        mesh=mesh,
        in_specs=(
            P(None, ("pulse", "tile"), None),
            P(),
            P(("pulse", "tile")),
            P(("pulse", "tile")),
            P(("pulse", "tile")),
            P(("pulse", "tile"), None),
            P(None, ("pulse", "tile")),
        ),
        out_specs=P(None, "pulse", "tile"),
        check_vma=False,
    )
```

```python
import functools

import jax
import jax.numpy as jnp
from jax import lax
from jax.experimental import pallas as pl
from jax.experimental.pallas import tpu as pltpu
from jax.sharding import PartitionSpec as P

F32 = jnp.float32
BF16 = jnp.bfloat16
MESH = pl.DeviceIdType.MESH
LANES = 128
DOP_SPLIT = 32
VMEM_LIMIT = 60 * 1024 * 1024


def spread(meta, field, rows8, n_rows):
    lane = lax.broadcasted_iota(jnp.int32, (meta.shape[1], n_rows), 0)
    col = lax.broadcasted_iota(jnp.int32, (meta.shape[1], n_rows), 1)
    pick = (lane == field * rows8 + col % rows8).astype(F32).astype(BF16)
    wide = jnp.dot(meta, pick, preferred_element_type=F32)
    owner = lax.broadcasted_iota(jnp.int32, wide.shape, 0)
    column = lax.broadcasted_iota(jnp.int32, wide.shape, 1)
    return jnp.sum(jnp.where(owner == column // rows8, wide, 0.0), axis=0, keepdims=True)


def thirds(x):
    a = x.astype(BF16)
    rest = x - a.astype(F32)
    b = rest.astype(BF16)
    return [a, b, (rest - b.astype(F32)).astype(BF16)]


def swap_parts(v, part1, p_dev):
    n = v.shape[-1]
    return jnp.where(part1, pltpu.roll(v, p_dev, 1), pltpu.roll(v, n - p_dev, 1))


def focus_kernel(
    n_pulse, n_tile, r_dev,
    off_ref, fine_ref, dop_ref, order_ref, idx_ref, raw_ref, filt_ref,
    left_ref, bands_ref,
    win_ref, meta_ref, scal_ref, filt_buf, x_ref, prof_ref, cut_ref, out_buf, g_ref, got_ref,
    f_sem, s_sem, z_send, z_recv, t_send, t_recv, p_send, p_recv, g_send, g_recv,
):
    me_p = lax.axis_index("pulse")
    me_t = lax.axis_index("tile")
    half = n_tile // 2
    core = me_t % 2
    chip = me_t // 2
    partner = chip * 2 + (1 - core)
    p_dev = raw_ref.shape[1]
    steps = order_ref.shape[1]
    raw_len = raw_ref.shape[2]
    win = x_ref.shape[2]
    rows = x_ref.shape[1]
    rows8 = 2 * p_dev
    n_dev = n_pulse * half
    n_rows = 2 * rows
    chunks, chunk = filt_buf.shape[0], filt_buf.shape[3]
    stride = prof_ref.shape[0] // rows
    band = bands_ref.shape[3]
    pieces = band // LANES

    def pulse_peer(d):
        return (lax.rem(me_p + d, n_pulse), me_t)

    def tile_peer(d):
        return (me_p, lax.rem(chip + d, half) * 2 + core)

    def any_tile(d):
        return (me_p, lax.rem(me_t + d, n_tile))

    barrier = pltpu.get_barrier_semaphore()
    for d in range(1, n_pulse):
        pl.semaphore_signal(barrier, 1, device_id=pulse_peer(d), device_id_type=MESH)
    for d in range(1, n_tile):
        pl.semaphore_signal(barrier, 1, device_id=any_tile(d), device_id_type=MESH)

    def load_filter(n):
        return pltpu.make_async_copy(
            filt_ref.at[:, :, pl.ds(n * chunk, chunk)], filt_buf.at[n], f_sem.at[n]
        )

    for n in range(chunks):
        load_filter(n).start()

    raw = jnp.concatenate([raw_ref[0].astype(F32), raw_ref[1].astype(F32)], 0)
    row = lax.broadcasted_iota(jnp.int32, (rows8, win), 0)
    cut = jnp.zeros((rows8, win), F32)
    for p in range(p_dev):
        off = off_ref[p]
        shift = jnp.where(off == 0, 0, raw_len - off)
        turned = pltpu.roll(raw, shift, 1)[:, :win]
        cut = jnp.where(row % p_dev == p, turned, cut)
    mine = me_p * half + chip
    win_ref[mine] = cut.astype(BF16)
    lane = lax.broadcasted_iota(jnp.int32, meta_ref.shape[2:], 1)
    line = jnp.zeros(meta_ref.shape[2:], jnp.int32)
    for p in range(p_dev):
        pulse_lane = (lane < 4 * rows8) & (lane % p_dev == p)
        line = jnp.where(pulse_lane & (lane // rows8 == 1), fine_ref[p], line)
        line = jnp.where(pulse_lane & (lane // rows8 == 2), dop_ref[p] % DOP_SPLIT, line)
        line = jnp.where(pulse_lane & (lane // rows8 == 3), dop_ref[p] // DOP_SPLIT, line)
        line = jnp.where((lane < rows8) & (lane % p_dev == order_ref[0, p]), p, line)
        for t in range(n_tile):
            line = jnp.where(lane == 4 * rows8 + t * p_dev + p, idx_ref[t, p], line)
    meta_ref[core, mine] = line
    pl.semaphore_wait(barrier, n_pulse - 1 + n_tile - 1)

    def copies(slot, send, recv, at, target):
        return [
            pltpu.make_async_remote_copy(
                src_ref=ref, dst_ref=ref, send_sem=send.at[(a,) + at], recv_sem=recv.at[(a,) + at],
                device_id=target, device_id_type=MESH,
            )
            for a, ref in enumerate((win_ref.at[slot], meta_ref.at[core, slot]))
        ]

    started = []

    def send(*args):
        for c in copies(*args):
            c.start()
            started.append(c)

    def arrive(*args):
        for c in copies(*args):
            c.wait_recv()

    for d in reversed(range(1, n_pulse)):
        send(mine, z_send, z_recv, (d,), pulse_peer(d))
    for dp in range(n_pulse):
        slot = lax.rem(me_p + n_pulse - dp, n_pulse) * half + chip
        if dp:
            arrive(slot, z_send, z_recv, (dp,), pulse_peer(dp))
        for dt in reversed(range(1, half)):
            send(slot, t_send, t_recv, (dp, dt), tile_peer(dt))
    for dp in range(n_pulse):
        for dt in range(1, half):
            slot = lax.rem(me_p + n_pulse - dp, n_pulse) * half + lax.rem(chip + half - dt, half)
            arrive(slot, t_send, t_recv, (dp, dt), tile_peer(dt))

    to_scalar = pltpu.make_async_copy(meta_ref.at[core], scal_ref, s_sem)
    to_scalar.start()
    meta_move = pltpu.make_async_remote_copy(
        src_ref=meta_ref.at[core], dst_ref=meta_ref.at[core],
        send_sem=p_send.at[2], recv_sem=p_recv.at[2],
        device_id=(me_p, partner), device_id_type=MESH,
    )
    meta_move.start()
    x = win_ref[...].astype(F32)
    r = lax.broadcasted_iota(jnp.int32, x.shape, 1)
    y = jnp.where(r < p_dev, -1.0, 1.0) * pltpu.roll(x, p_dev, 1)
    x_ref[0] = x.reshape(rows, win).astype(BF16)
    x_ref[1] = y.reshape(rows, win).astype(BF16)

    def compress(n, carry):
        load_filter(n).wait()
        acc = jnp.dot(x_ref[0], filt_buf[n, 0], preferred_element_type=F32) + jnp.dot(
            x_ref[1], filt_buf[n, 1], preferred_element_type=F32
        )
        acc = acc.astype(BF16).astype(F32)
        for c in range(chunk // LANES):
            prof_ref[pl.ds(n * (chunk // LANES) + c, rows, stride=stride), :] = acc[
                :, c * LANES : (c + 1) * LANES
            ]
        return carry

    lax.fori_loop(0, chunks, compress, 0)
    to_scalar.wait()
    lane8 = lax.broadcasted_iota(jnp.int32, (pieces, LANES), 1)

    def cut_bands(tile):
        def owner(d, carry):
            for p in range(p_dev):
                start = scal_ref[d, 0, 4 * rows8 + tile * p_dev + p]
                q = start >> 7
                r = start & (LANES - 1)
                turn = (LANES - r) & (LANES - 1)
                keep = lane8 < LANES - r
                for part in range(2):
                    row = d * rows8 + part * p_dev + p
                    low = pltpu.roll(prof_ref[pl.ds(row * stride + q, pieces), :], turn, 1)
                    high = pltpu.roll(prof_ref[pl.ds(row * stride + q + 1, pieces), :], turn, 1)
                    here = jnp.where(keep, low, high)
                    after = pltpu.roll(jnp.where(lane8 == 0, high, here), LANES - 1, 1)
                    cut_ref[pl.ds(row * pieces, pieces), :] = here
                    cut_ref[pl.ds((rows + row) * pieces, pieces), :] = after
            return carry

        lax.fori_loop(0, n_dev, owner, 0, unroll=4)

    cut_bands(partner)
    for c in range(pieces):
        for b in range(2):
            out_buf[b, :, c * LANES : (c + 1) * LANES] = cut_ref[
                pl.ds(b * rows * pieces + c, rows, stride=pieces), :
            ].astype(BF16)
    band_moves = [
        pltpu.make_async_remote_copy(
            src_ref=out_buf.at[b], dst_ref=bands_ref.at[b, core],
            send_sem=p_send.at[b], recv_sem=p_recv.at[b],
            device_id=(me_p, partner), device_id_type=MESH,
        )
        for b in range(2)
    ]
    for move in band_moves:
        move.start()
    cut_bands(me_t)
    for c in range(pieces):
        for b in range(2):
            bands_ref[b, core, :, c * LANES : (c + 1) * LANES] = cut_ref[
                pl.ds(b * rows * pieces + c, rows, stride=pieces), :
            ].astype(BF16)
    pltpu.make_async_remote_copy(
        src_ref=meta_ref.at[1 - core], dst_ref=meta_ref.at[1 - core],
        send_sem=p_send.at[2], recv_sem=p_recv.at[2],
        device_id=(me_p, partner), device_id_type=MESH,
    ).wait_recv()
    meta = meta_ref[...].reshape(2 * n_dev, meta_ref.shape[3]).astype(F32).astype(BF16)
    blk = spread(meta, 0, rows8, n_rows)
    fine = spread(meta, 1, rows8, n_rows) * (1.0 / 16.0)
    dop = spread(meta, 2, rows8, n_rows) + DOP_SPLIT * spread(meta, 3, rows8, n_rows)
    sel = lax.broadcasted_iota(jnp.int32, (2 * steps, n_rows), 0)
    col = lax.broadcasted_iota(jnp.int32, (2 * steps, n_rows), 1)
    in_block = (sel // 2).astype(F32) == blk
    same = in_block & (sel % 2 == (col % rows8) // p_dev)
    zero = jnp.zeros((2 * steps, n_rows), F32)
    p_left = jnp.concatenate([jnp.where(same, 1.0 - fine, zero), jnp.where(same, fine, zero)], 1)
    q_left = jnp.concatenate([jnp.where(same, -1.0, zero), jnp.where(same, 1.0, zero)], 1)
    left = jnp.concatenate([p_left, q_left], 0).astype(BF16)
    for b in range(2):
        pltpu.make_async_remote_copy(
            src_ref=out_buf.at[b], dst_ref=bands_ref.at[b, 1 - core],
            send_sem=p_send.at[b], recv_sem=p_recv.at[b],
            device_id=(me_p, partner), device_id_type=MESH,
        ).wait_recv()
    bands = bands_ref[...].reshape(2 * n_rows, band)
    pq = jnp.dot(left, bands, preferred_element_type=F32)
    k = 2 * steps
    x = 4.0 * pq[:k] + 1.5 * pq[k:]
    y = 1.5 * pq[:k] + 0.875 * pq[k:]
    xs = jnp.concatenate(thirds(x) + thirds(y), 0)
    d6 = lax.dot_general(xs, bands, (((1,), (1,)), ((), ())), preferred_element_type=F32)
    dx = d6[2 * k : 3 * k] + d6[k : 2 * k] + d6[:k]
    dy = d6[5 * k : 6 * k] + d6[4 * k : 5 * k] + d6[3 * k : 4 * k]
    h = ((1.0 - fine) * dx[:, :n_rows] - dy[:, :n_rows]) + (
        fine * dx[:, n_rows:] + dy[:, n_rows:]
    )
    hr = jnp.sum(jnp.where(in_block & (sel % 2 == 0), h, 0.0), axis=0, keepdims=True)
    hi = jnp.sum(jnp.where(in_block & (sel % 2 == 1), h, 0.0), axis=0, keepdims=True)
    both = jnp.concatenate([hr, hi, jnp.zeros((6, n_rows), F32)], 0)
    part1 = (lax.broadcasted_iota(jnp.int32, (8, n_rows), 1) % rows8) >= p_dev
    other = swap_parts(both, part1, p_dev)
    hr, hi, hr_o, hi_o = both[0:1], both[1:2], other[0:1], other[1:2]
    one = part1[0:1]
    g_ref[0:1] = jnp.where(one, hr_o + hi, hr + hi_o)
    g_ref[1:2] = jnp.where(one, hr - hi_o, hr_o - hi)
    g_moves = [
        pltpu.make_async_remote_copy(
            src_ref=g_ref, dst_ref=got_ref.at[d],
            send_sem=g_send.at[d], recv_sem=g_recv.at[d],
            device_id=any_tile(d), device_id_type=MESH,
        )
        for d in range(1, n_tile)
    ]
    for move in g_moves:
        move.start()
    total_rows = r_dev * n_pulse
    image_row = me_p * r_dev + lax.broadcasted_iota(jnp.int32, (r_dev, n_rows), 0)
    turns = dop.astype(jnp.int32) * image_row
    if total_rows & (total_rows - 1):
        turns = turns % total_rows
    else:
        turns = turns & (total_rows - 1)
    angle = 2.0 * jnp.pi * turns.astype(F32) / total_rows
    norm = 1.0 / jnp.sqrt(F32(n_rows // 2))
    er = (jnp.cos(angle) * norm).astype(BF16).astype(F32)
    ei = (jnp.sin(angle) * norm).astype(BF16).astype(F32)
    total = g_ref[...]
    for d in range(1, n_tile):
        g_moves[d - 1].wait_recv()
        total = total + got_ref[d]
    g_re, g_im = total[0:1], total[1:2]
    scale = jnp.sqrt(g_re * g_re + g_im * g_im + 1.0)
    c_re = g_re / scale
    c_im = -g_im / scale
    alpha = jnp.where(one, -c_im, c_re)
    beta = jnp.where(one, c_re, c_im)
    w = (er * alpha - ei * beta, er * beta + ei * alpha)
    for z in range(2):
        here = pl.ds(z * r_dev, r_dev)
        left_ref[0, here, :n_rows] = (w[z] * (1.0 - fine)).astype(BF16)
        left_ref[0, here, n_rows:] = (w[z] * fine).astype(BF16)
        left_ref[1, here, :n_rows] = (w[z] * -fine).astype(BF16)
        left_ref[1, here, n_rows:] = (w[z] * (1.0 + fine)).astype(BF16)
    for c in started + [meta_move] + band_moves + g_moves:
        c.wait_send()


def focus(n_pulse, n_tile, r_dev, band, range_off, fine, dop, order, idx, raw, filt):
    p_dev = raw.shape[1]
    win, ups = filt.shape[1:]
    half = n_tile // 2
    n_dev = n_pulse * half
    rows = n_dev * 2 * p_dev
    n_rows = 2 * rows
    fields = 8 * p_dev + idx.size
    width = fields + -fields % LANES
    chunk = 2 * LANES
    sem = pltpu.SemaphoreType.DMA
    return pl.pallas_call(
        functools.partial(focus_kernel, n_pulse, n_tile, r_dev),
        out_shape=(
            jax.ShapeDtypeStruct((2, 2 * r_dev, 2 * n_rows), BF16),
            jax.ShapeDtypeStruct((2, 2, rows, band), BF16),
        ),
        in_specs=[pl.BlockSpec(memory_space=pltpu.SMEM)] * 5
        + [pl.BlockSpec(memory_space=pltpu.VMEM), pl.BlockSpec(memory_space=pl.ANY)],
        out_specs=[pl.BlockSpec(memory_space=pltpu.VMEM)] * 2,
        scratch_shapes=[
            pltpu.VMEM((n_dev, 2 * p_dev, win), BF16),
            pltpu.VMEM((2, n_dev, 1, width), jnp.int32),
            pltpu.SMEM((n_dev, 1, width), jnp.int32),
            pltpu.VMEM((ups // chunk, 2, win, chunk), BF16),
            pltpu.VMEM((2, rows, win), BF16),
            pltpu.VMEM((rows * (ups // LANES) + 8, LANES), F32),
            pltpu.VMEM((2 * rows * (band // LANES), LANES), F32),
            pltpu.VMEM((2, rows, band), BF16),
            pltpu.VMEM((2, n_rows), F32),
            pltpu.VMEM((n_tile, 2, n_rows), F32),
            sem((ups // chunk,)),
            sem,
            sem((2, n_pulse)),
            sem((2, n_pulse)),
            sem((2, n_pulse, half)),
            sem((2, n_pulse, half)),
            sem((3,)),
            sem((3,)),
            sem((n_tile,)),
            sem((n_tile,)),
        ],
        compiler_params=pltpu.CompilerParams(
            collective_id=0, has_side_effects=True, vmem_limit_bytes=VMEM_LIMIT
        ),
    )(range_off, fine, dop, order, idx, raw, filt)


def image_kernel(left_ref, bands_ref, out_ref, up_ref):
    r_dev = out_ref.shape[1]
    width = bands_ref.shape[1]
    out_chunk = 4 * LANES
    j = lax.broadcasted_iota(jnp.int32, up_ref.shape, 0)
    c = lax.broadcasted_iota(jnp.int32, up_ref.shape, 1)
    w = (c % 4).astype(F32) * 0.25
    up = jnp.where(j < LANES, 1.0 - w, w)
    up_ref[...] = jnp.where(j % LANES == c // 4, up, 0.0).astype(BF16)
    r0 = jnp.dot(left_ref[0], bands_ref[...], preferred_element_type=F32).astype(BF16)
    r1 = jnp.dot(left_ref[1], bands_ref[...], preferred_element_type=F32).astype(BF16)
    for s in range(width // LANES):
        cols = slice(s * LANES, (s + 1) * LANES)
        both = jnp.concatenate([r0[:, cols], r1[:, cols]], 1)
        res = jnp.dot(both, up_ref[...], preferred_element_type=F32).astype(BF16)
        for z in range(2):
            out_ref[z, :, s * out_chunk : (s + 1) * out_chunk] = res[z * r_dev : (z + 1) * r_dev]


def image(left, bands, r_dev):
    band = bands.shape[1]
    k = bands.shape[0]
    width = 2 * LANES
    return pl.pallas_call(
        image_kernel,
        grid=(band // width,),
        out_shape=jax.ShapeDtypeStruct((2, r_dev, 4 * band), BF16),
        in_specs=[
            pl.BlockSpec(left.shape, lambda i: (0, 0, 0)),
            pl.BlockSpec((k, width), lambda i: (0, i)),
        ],
        out_specs=pl.BlockSpec((2, r_dev, 4 * width), lambda i: (0, 0, i)),
        scratch_shapes=[pltpu.VMEM((2 * LANES, 4 * LANES), BF16)],
        compiler_params=pltpu.CompilerParams(vmem_limit_bytes=VMEM_LIMIT),
    )(left, bands)


BAND = 1024
R_DEV = 128


def shards(raw, filt, range_off, fine, dop, pulse_order, band_idx):
    n_pulse = lax.axis_size("pulse")
    n_tile = lax.axis_size("tile")
    left, bands = focus(
        n_pulse, n_tile, R_DEV, BAND, range_off, fine, dop, pulse_order, band_idx, raw, filt
    )
    bands = bands.reshape(-1, BAND)
    return image(left, bands, R_DEV)


def solution(mesh):
    return jax.shard_map(
        shards,
        mesh=mesh,
        in_specs=(
            P(None, ("pulse", "tile"), None),
            P(),
            P(("pulse", "tile")),
            P(("pulse", "tile")),
            P(("pulse", "tile")),
            P(("pulse", "tile"), None),
            P(None, ("pulse", "tile")),
        ),
        out_specs=P(None, "pulse", "tile"),
        check_vma=False,
    )
```

```python
import functools

import jax
import jax.numpy as jnp
from jax import lax
from jax.experimental import pallas as pl
from jax.experimental.pallas import tpu as pltpu
from jax.sharding import PartitionSpec as P

F32 = jnp.float32
BF16 = jnp.bfloat16
MESH = pl.DeviceIdType.MESH
LANES = 128
DOP_SPLIT = 32
VMEM_LIMIT = 44 * 1024 * 1024


def spread(meta, field, rows8, n_rows):
    lane = lax.broadcasted_iota(jnp.int32, (meta.shape[1], n_rows), 0)
    col = lax.broadcasted_iota(jnp.int32, (meta.shape[1], n_rows), 1)
    pick = (lane == field * rows8 + col % rows8).astype(F32).astype(BF16)
    wide = jnp.dot(meta, pick, preferred_element_type=F32)
    owner = lax.broadcasted_iota(jnp.int32, wide.shape, 0)
    column = lax.broadcasted_iota(jnp.int32, wide.shape, 1)
    return jnp.sum(jnp.where(owner == column // rows8, wide, 0.0), axis=0, keepdims=True)


def thirds(x):
    a = x.astype(BF16)
    rest = x - a.astype(F32)
    b = rest.astype(BF16)
    return [a, b, (rest - b.astype(F32)).astype(BF16)]


def swap_parts(v, part1, p_dev):
    n = v.shape[-1]
    return jnp.where(part1, pltpu.roll(v, p_dev, 1), pltpu.roll(v, n - p_dev, 1))


def focus_kernel(
    n_pulse, n_tile, r_dev,
    off_ref, fine_ref, dop_ref, order_ref, idx_ref, raw_ref, filt_ref,
    left_ref, samp_ref,
    bands_ref, up_ref, win_ref, meta_ref, scal_ref, filt_buf, x_ref, prof_ref, cut_ref, out_buf, g_ref, got_ref,
    f_sem, s_sem, z_send, z_recv, t_send, t_recv, p_send, p_recv, g_send, g_recv,
):
    me_p = lax.axis_index("pulse")
    me_t = lax.axis_index("tile")
    half = n_tile // 2
    core = me_t % 2
    chip = me_t // 2
    partner = chip * 2 + (1 - core)
    p_dev = raw_ref.shape[1]
    steps = order_ref.shape[1]
    raw_len = raw_ref.shape[2]
    win = x_ref.shape[2]
    rows = x_ref.shape[1]
    rows8 = 2 * p_dev
    n_dev = n_pulse * half
    n_rows = 2 * rows
    chunks, chunk = filt_buf.shape[0], filt_buf.shape[3]
    stride = prof_ref.shape[0] // rows
    band = bands_ref.shape[3]
    pieces = band // LANES

    def pulse_peer(d):
        return (lax.rem(me_p + d, n_pulse), me_t)

    def tile_peer(d):
        return (me_p, lax.rem(chip + d, half) * 2 + core)

    def any_tile(d):
        return (me_p, lax.rem(me_t + d, n_tile))

    barrier = pltpu.get_barrier_semaphore()
    for d in range(1, n_pulse):
        pl.semaphore_signal(barrier, 1, device_id=pulse_peer(d), device_id_type=MESH)
    for d in range(1, n_tile):
        pl.semaphore_signal(barrier, 1, device_id=any_tile(d), device_id_type=MESH)

    def load_filter(n):
        return pltpu.make_async_copy(
            filt_ref.at[:, :, pl.ds(n * chunk, chunk)], filt_buf.at[n], f_sem.at[n]
        )

    for n in range(chunks):
        load_filter(n).start()

    raw = jnp.concatenate([raw_ref[0].astype(F32), raw_ref[1].astype(F32)], 0)
    row = lax.broadcasted_iota(jnp.int32, (rows8, win), 0)
    cut = jnp.zeros((rows8, win), F32)
    for p in range(p_dev):
        off = off_ref[p]
        shift = jnp.where(off == 0, 0, raw_len - off)
        turned = pltpu.roll(raw, shift, 1)[:, :win]
        cut = jnp.where(row % p_dev == p, turned, cut)
    mine = me_p * half + chip
    win_ref[mine] = cut.astype(BF16)
    lane = lax.broadcasted_iota(jnp.int32, meta_ref.shape[2:], 1)
    line = jnp.zeros(meta_ref.shape[2:], jnp.int32)
    for p in range(p_dev):
        pulse_lane = (lane < 4 * rows8) & (lane % p_dev == p)
        line = jnp.where(pulse_lane & (lane // rows8 == 1), fine_ref[p], line)
        line = jnp.where(pulse_lane & (lane // rows8 == 2), dop_ref[p] % DOP_SPLIT, line)
        line = jnp.where(pulse_lane & (lane // rows8 == 3), dop_ref[p] // DOP_SPLIT, line)
        line = jnp.where((lane < rows8) & (lane % p_dev == order_ref[0, p]), p, line)
        for t in range(n_tile):
            line = jnp.where(lane == 4 * rows8 + t * p_dev + p, idx_ref[p, t], line)
    meta_ref[core, mine] = line
    j = lax.broadcasted_iota(jnp.int32, up_ref.shape, 0)
    c = lax.broadcasted_iota(jnp.int32, up_ref.shape, 1)
    w = (c % 4).astype(F32) * 0.25
    up = jnp.where(j < LANES, 1.0 - w, w)
    up_ref[...] = jnp.where(j % LANES == c // 4, up, 0.0).astype(BF16)
    pl.semaphore_wait(barrier, n_pulse - 1 + n_tile - 1)

    def copies(slot, send, recv, at, target):
        return [
            pltpu.make_async_remote_copy(
                src_ref=ref, dst_ref=ref, send_sem=send.at[(a,) + at], recv_sem=recv.at[(a,) + at],
                device_id=target, device_id_type=MESH,
            )
            for a, ref in enumerate((win_ref.at[slot], meta_ref.at[core, slot]))
        ]

    started = []

    def send(*args):
        for c in copies(*args):
            c.start()
            started.append(c)

    def arrive(*args):
        for c in copies(*args):
            c.wait_recv()

    for d in reversed(range(1, n_pulse)):
        send(mine, z_send, z_recv, (d,), pulse_peer(d))
    for dp in range(n_pulse):
        slot = lax.rem(me_p + n_pulse - dp, n_pulse) * half + chip
        if dp:
            arrive(slot, z_send, z_recv, (dp,), pulse_peer(dp))
        for dt in reversed(range(1, half)):
            send(slot, t_send, t_recv, (dp, dt), tile_peer(dt))
    for dp in range(n_pulse):
        for dt in range(1, half):
            slot = lax.rem(me_p + n_pulse - dp, n_pulse) * half + lax.rem(chip + half - dt, half)
            arrive(slot, t_send, t_recv, (dp, dt), tile_peer(dt))

    to_scalar = pltpu.make_async_copy(meta_ref.at[core], scal_ref, s_sem)
    to_scalar.start()
    meta_move = pltpu.make_async_remote_copy(
        src_ref=meta_ref.at[core], dst_ref=meta_ref.at[core],
        send_sem=p_send.at[2], recv_sem=p_recv.at[2],
        device_id=(me_p, partner), device_id_type=MESH,
    )
    meta_move.start()
    x = win_ref[...].astype(F32)
    r = lax.broadcasted_iota(jnp.int32, x.shape, 1)
    y = jnp.where(r < p_dev, -1.0, 1.0) * pltpu.roll(x, p_dev, 1)
    x_ref[0] = x.reshape(rows, win).astype(BF16)
    x_ref[1] = y.reshape(rows, win).astype(BF16)

    def compress(n, carry):
        load_filter(n).wait()
        acc = jnp.dot(x_ref[0], filt_buf[n, 0], preferred_element_type=F32) + jnp.dot(
            x_ref[1], filt_buf[n, 1], preferred_element_type=F32
        )
        acc = acc.astype(BF16).astype(F32)
        for c in range(chunk // LANES):
            prof_ref[pl.ds(n * (chunk // LANES) + c, rows, stride=stride), :] = acc[
                :, c * LANES : (c + 1) * LANES
            ]
        return carry

    lax.fori_loop(0, chunks, compress, 0, unroll=2)
    to_scalar.wait()
    lane8 = lax.broadcasted_iota(jnp.int32, (pieces, LANES), 1)

    def cut_bands(tile):
        def owner(d, carry):
            for p in range(p_dev):
                start = scal_ref[d, 0, 4 * rows8 + tile * p_dev + p]
                q = start >> 7
                r = start & (LANES - 1)
                turn = (LANES - r) & (LANES - 1)
                keep = lane8 < LANES - r
                for part in range(2):
                    row = d * rows8 + part * p_dev + p
                    low = pltpu.roll(prof_ref[pl.ds(row * stride + q, pieces), :], turn, 1)
                    high = pltpu.roll(prof_ref[pl.ds(row * stride + q + 1, pieces), :], turn, 1)
                    here = jnp.where(keep, low, high)
                    after = pltpu.roll(jnp.where(lane8 == 0, high, here), LANES - 1, 1)
                    cut_ref[pl.ds(row * pieces, pieces), :] = here
                    cut_ref[pl.ds((rows + row) * pieces, pieces), :] = after
            return carry

        lax.fori_loop(0, n_dev, owner, 0, unroll=4)

    cut_bands(partner)
    for c in range(pieces):
        for b in range(2):
            out_buf[b, :, c * LANES : (c + 1) * LANES] = cut_ref[
                pl.ds(b * rows * pieces + c, rows, stride=pieces), :
            ].astype(BF16)
    band_moves = [
        pltpu.make_async_remote_copy(
            src_ref=out_buf.at[b], dst_ref=bands_ref.at[b, core],
            send_sem=p_send.at[b], recv_sem=p_recv.at[b],
            device_id=(me_p, partner), device_id_type=MESH,
        )
        for b in range(2)
    ]
    for move in band_moves:
        move.start()
    cut_bands(me_t)
    for c in range(pieces):
        for b in range(2):
            bands_ref[b, core, :, c * LANES : (c + 1) * LANES] = cut_ref[
                pl.ds(b * rows * pieces + c, rows, stride=pieces), :
            ].astype(BF16)
    pltpu.make_async_remote_copy(
        src_ref=meta_ref.at[1 - core], dst_ref=meta_ref.at[1 - core],
        send_sem=p_send.at[2], recv_sem=p_recv.at[2],
        device_id=(me_p, partner), device_id_type=MESH,
    ).wait_recv()
    meta = meta_ref[...].reshape(2 * n_dev, meta_ref.shape[3]).astype(F32).astype(BF16)
    blk = spread(meta, 0, rows8, n_rows)
    fine = spread(meta, 1, rows8, n_rows) * (1.0 / 16.0)
    dop = spread(meta, 2, rows8, n_rows) + DOP_SPLIT * spread(meta, 3, rows8, n_rows)
    sel = lax.broadcasted_iota(jnp.int32, (2 * steps, n_rows), 0)
    col = lax.broadcasted_iota(jnp.int32, (2 * steps, n_rows), 1)
    in_block = (sel // 2).astype(F32) == blk
    same = in_block & (sel % 2 == (col % rows8) // p_dev)
    zero = jnp.zeros((2 * steps, n_rows), F32)
    p_left = jnp.concatenate([jnp.where(same, 1.0 - fine, zero), jnp.where(same, fine, zero)], 1)
    q_left = jnp.concatenate([jnp.where(same, -1.0, zero), jnp.where(same, 1.0, zero)], 1)
    left = jnp.concatenate([p_left, q_left], 0).astype(BF16)
    for b in range(2):
        pltpu.make_async_remote_copy(
            src_ref=out_buf.at[b], dst_ref=bands_ref.at[b, 1 - core],
            send_sem=p_send.at[b], recv_sem=p_recv.at[b],
            device_id=(me_p, partner), device_id_type=MESH,
        ).wait_recv()
    bands = bands_ref[...].reshape(2 * n_rows, band)
    pq = jnp.dot(left, bands, preferred_element_type=F32)
    k = 2 * steps
    x = 4.0 * pq[:k] + 1.5 * pq[k:]
    y = 1.5 * pq[:k] + 0.875 * pq[k:]
    xs = jnp.concatenate(thirds(x) + thirds(y), 0)
    d6 = lax.dot_general(xs, bands, (((1,), (1,)), ((), ())), preferred_element_type=F32)
    dx = d6[2 * k : 3 * k] + d6[k : 2 * k] + d6[:k]
    dy = d6[5 * k : 6 * k] + d6[4 * k : 5 * k] + d6[3 * k : 4 * k]
    h = ((1.0 - fine) * dx[:, :n_rows] - dy[:, :n_rows]) + (
        fine * dx[:, n_rows:] + dy[:, n_rows:]
    )
    hr = jnp.sum(jnp.where(in_block & (sel % 2 == 0), h, 0.0), axis=0, keepdims=True)
    hi = jnp.sum(jnp.where(in_block & (sel % 2 == 1), h, 0.0), axis=0, keepdims=True)
    both = jnp.concatenate([hr, hi, jnp.zeros((6, n_rows), F32)], 0)
    part1 = (lax.broadcasted_iota(jnp.int32, (8, n_rows), 1) % rows8) >= p_dev
    other = swap_parts(both, part1, p_dev)
    hr, hi, hr_o, hi_o = both[0:1], both[1:2], other[0:1], other[1:2]
    one = part1[0:1]
    g_ref[0:1] = jnp.where(one, hr_o + hi, hr + hi_o)
    g_ref[1:2] = jnp.where(one, hr - hi_o, hr_o - hi)
    g_moves = [
        pltpu.make_async_remote_copy(
            src_ref=g_ref, dst_ref=got_ref.at[d],
            send_sem=g_send.at[d], recv_sem=g_recv.at[d],
            device_id=any_tile(d), device_id_type=MESH,
        )
        for d in range(1, n_tile)
    ]
    for move in g_moves:
        move.start()
    total_rows = r_dev * n_pulse
    image_row = me_p * r_dev + lax.broadcasted_iota(jnp.int32, (r_dev, n_rows), 0)
    turns = dop.astype(jnp.int32) * image_row
    if total_rows & (total_rows - 1):
        turns = turns % total_rows
    else:
        turns = turns & (total_rows - 1)
    angle = 2.0 * jnp.pi * turns.astype(F32) / total_rows
    norm = 1.0 / jnp.sqrt(F32(n_rows // 2))
    er = (jnp.cos(angle) * norm).astype(BF16).astype(F32)
    ei = (jnp.sin(angle) * norm).astype(BF16).astype(F32)
    square = (n_rows, n_rows)
    diagonal = lax.broadcasted_iota(jnp.int32, square, 0) == lax.broadcasted_iota(jnp.int32, square, 1)
    fine_col = jnp.sum(jnp.where(diagonal, fine, 0.0), axis=1, keepdims=True)
    for s in range(pieces):
        cols = slice(s * LANES, (s + 1) * LANES)
        b0 = bands_ref[0, :, :, cols].reshape(n_rows, LANES).astype(F32)
        b1 = bands_ref[1, :, :, cols].reshape(n_rows, LANES).astype(F32)
        bend = fine_col * (b1 - b0)
        pair = jnp.concatenate([b0 + bend, b1 + bend], 1).astype(BF16)
        samp_ref[:, 4 * s * LANES : 4 * (s + 1) * LANES] = jnp.dot(
            pair, up_ref[...], preferred_element_type=F32
        ).astype(BF16)
    total = g_ref[...]
    for d in range(1, n_tile):
        g_moves[d - 1].wait_recv()
        total = total + got_ref[d]
    g_re, g_im = total[0:1], total[1:2]
    scale = jnp.sqrt(g_re * g_re + g_im * g_im + 1.0)
    c_re = g_re / scale
    c_im = -g_im / scale
    alpha = jnp.where(one, -c_im, c_re)
    beta = jnp.where(one, c_re, c_im)
    w = (er * alpha - ei * beta, er * beta + ei * alpha)
    for z in range(2):
        here = pl.ds(z * r_dev, r_dev)
        left_ref[here, :] = w[z].astype(BF16)
    for c in started + [meta_move] + band_moves + g_moves:
        c.wait_send()


def focus(n_pulse, n_tile, r_dev, band, range_off, fine, dop, order, idx, raw, filt):
    p_dev = raw.shape[1]
    win, ups = filt.shape[1:]
    half = n_tile // 2
    n_dev = n_pulse * half
    rows = n_dev * 2 * p_dev
    n_rows = 2 * rows
    fields = 8 * p_dev + idx.size
    width = fields + -fields % LANES
    chunk = 2 * LANES
    sem = pltpu.SemaphoreType.DMA
    return pl.pallas_call(
        functools.partial(focus_kernel, n_pulse, n_tile, r_dev),
        out_shape=(
            jax.ShapeDtypeStruct((2 * r_dev, n_rows), BF16),
            jax.ShapeDtypeStruct((n_rows, 4 * band), BF16),
        ),
        in_specs=[pl.BlockSpec(memory_space=pltpu.SMEM)] * 5
        + [pl.BlockSpec(memory_space=pltpu.VMEM), pl.BlockSpec(memory_space=pl.ANY)],
        out_specs=[pl.BlockSpec(memory_space=pltpu.VMEM)] * 2,
        scratch_shapes=[
            pltpu.VMEM((2, 2, rows, band), BF16),
            pltpu.VMEM((2 * LANES, 4 * LANES), BF16),
            pltpu.VMEM((n_dev, 2 * p_dev, win), BF16),
            pltpu.VMEM((2, n_dev, 1, width), jnp.int32),
            pltpu.SMEM((n_dev, 1, width), jnp.int32),
            pltpu.VMEM((ups // chunk, 2, win, chunk), BF16),
            pltpu.VMEM((2, rows, win), BF16),
            pltpu.VMEM((rows * (ups // LANES) + 8, LANES), F32),
            pltpu.VMEM((2 * rows * (band // LANES), LANES), F32),
            pltpu.VMEM((2, rows, band), BF16),
            pltpu.VMEM((2, n_rows), F32),
            pltpu.VMEM((n_tile, 2, n_rows), F32),
            sem((ups // chunk,)),
            sem,
            sem((2, n_pulse)),
            sem((2, n_pulse)),
            sem((2, n_pulse, half)),
            sem((2, n_pulse, half)),
            sem((3,)),
            sem((3,)),
            sem((n_tile,)),
            sem((n_tile,)),
        ],
        compiler_params=pltpu.CompilerParams(
            collective_id=0, has_side_effects=True, vmem_limit_bytes=VMEM_LIMIT
        ),
    )(range_off, fine, dop, order, idx, raw, filt)


def image_kernel(left_ref, samp_ref, out_ref):
    r_dev = out_ref.shape[1]
    res = jnp.dot(left_ref[...], samp_ref[...], preferred_element_type=F32).astype(BF16)
    for z in range(2):
        out_ref[z] = res[z * r_dev : (z + 1) * r_dev]


def image(left, samples, r_dev):
    k, cols = samples.shape
    width = cols // 4
    return pl.pallas_call(
        image_kernel,
        grid=(cols // width,),
        out_shape=jax.ShapeDtypeStruct((2, r_dev, cols), BF16),
        in_specs=[
            pl.BlockSpec(left.shape, lambda i: (0, 0)),
            pl.BlockSpec((k, width), lambda i: (0, i)),
        ],
        out_specs=pl.BlockSpec((2, r_dev, width), lambda i: (0, 0, i)),
        compiler_params=pltpu.CompilerParams(vmem_limit_bytes=VMEM_LIMIT),
    )(left, samples)


BAND = 1024
R_DEV = 128


def shards(raw, filt, range_off, fine, dop, pulse_order, band_idx):
    n_pulse = lax.axis_size("pulse")
    n_tile = lax.axis_size("tile")
    left, samples = focus(
        n_pulse, n_tile, R_DEV, BAND, range_off, fine, dop, pulse_order, band_idx.T, raw, filt
    )
    return image(left, samples, R_DEV)


def solution(mesh):
    return jax.shard_map(
        shards,
        mesh=mesh,
        in_specs=(
            P(None, ("pulse", "tile"), None),
            P(),
            P(("pulse", "tile")),
            P(("pulse", "tile")),
            P(("pulse", "tile")),
            P(("pulse", "tile"), None),
            P(None, ("pulse", "tile")),
        ),
        out_specs=P(None, "pulse", "tile"),
        check_vma=False,
    )
```
